32 devices in a mesh: parts: 1, grid: 32 (over z, y, x, core).
Axes of the slice: x: 2, y: 2, z: 4, core: 2. Of those that a mesh axis runs over, the one named last changes fastest.
Arguments:
- tokens: bfloat16 [128, 32, 1024], P(('parts', 'grid')), may hold values from -6 to 6
- cotangent: bfloat16 [128, 32, 1024], P(('parts', 'grid')), may hold values from -6 to 6
- w_sqkv: bfloat16 [1024, 3072], P('grid'), may hold values from -0.1875 to 0.1875
- w_so: bfloat16 [1024, 1024], P('grid'), may hold values from -0.1875 to 0.1875
- w_gqkv: bfloat16 [1024, 3072], P('grid'), may hold values from -0.1875 to 0.1875
- w_go: bfloat16 [1024, 1024], P('grid'), may hold values from -0.1875 to 0.1875
- keep: int32 [32, 128], P(None, 'parts'), may hold values from 0 to 1, as said below
Outputs:
- mixed: bfloat16 [128, 32, 1024], P(('parts', 'grid'))
- token_grad: bfloat16 [128, 32, 1024], P(('parts', 'grid'))
The draws below stay inside these ranges and needn't reach their ends.
Inputs may be any that keep to these rules, and one draw needn't show every extreme that they name: `keep`: every band group keeps at least one patch; the kept share differs from group to group.
All inputs are finite; a program needn't handle non-finite values.
Results may differ from the reference program's by a relative error of at most 0.017.
Values may be sent and summed in bfloat16 or wider, within the bound.
A program may use at most 192 MiB of HBM per device.

```python
from functools import partial
import jax
import jax.numpy as jnp
from jax import lax

D = 1024
H = 16
G = 32
P_SIZE = 128


def draw_keep(key, part):
    first = jax.random.fold_in(key, 11)
    second = jax.random.fold_in(key, 12)
    cutoff = jax.random.randint(first, (G, 1), 5, 85)
    noise = jax.random.randint(second, (G, P_SIZE), 0, 100)
    kept = (noise >= cutoff).astype(jnp.int32)
    forced = (jnp.arange(P_SIZE, dtype=jnp.int32)[None, :] % G == jnp.arange(G, dtype=jnp.int32)[:, None]).astype(jnp.int32)
    return jnp.maximum(kept, forced)


def levels(key, shape, shards, smallest, largest):
    factor_of, own = 1.0, jax.random.fold_in(key, 6)
    for axis_at, blocks in shards:
        draws = jnp.exp(jax.random.uniform(jax.random.fold_in(own, axis_at), (blocks,), jnp.float32, smallest / len(shards), largest / len(shards)))
        factor_of = factor_of * jnp.repeat(draws, shape[axis_at] // blocks).reshape([-1 if axis == axis_at else 1 for axis in range(len(shape))])
    return factor_of


def scatter_about(key, extent, deviation, bound, shards=(), held_as=jnp.bfloat16):
    drawn = deviation * jax.random.normal(key, extent, jnp.float32)
    if shards:
        drawn = drawn * levels(key, extent, shards, -0.22, 0.18)
    return jnp.clip(drawn, -bound, bound).astype(held_as)


def setup_inputs(seed: int = 0, part: int = 0) -> dict:
    seeds = jax.random.split(jax.random.key(seed), 8)
    part_splits = jax.random.split(jax.random.fold_in(seeds[7], part), 8)
    tokens = scatter_about(part_splits[0], (P_SIZE, G, D), 1.0, 6.0, ((0, 32),))
    cotangent = scatter_about(part_splits[1], (P_SIZE, G, D), 1.0, 6.0, ((0, 32),))
    w_sqkv = scatter_about(seeds[2], (D, 3 * D), D ** -0.5, 0.1875, ((0, 32),))
    w_so = scatter_about(seeds[3], (D, D), D ** -0.5, 0.1875, ((0, 32),))
    w_gqkv = scatter_about(seeds[4], (D, 3 * D), D ** -0.5, 0.1875, ((0, 32),))
    w_go = scatter_about(seeds[5], (D, D), D ** -0.5, 0.1875, ((0, 32),))
    keep = draw_keep(jax.random.fold_in(jax.random.fold_in(seeds[7], part), 71), part)
    return {"tokens": tokens, "cotangent": cotangent, "w_sqkv": w_sqkv, "w_so": w_so, "w_gqkv": w_gqkv, "w_go": w_go, "keep": keep}


def rms_normalize(values):
    wide = values.astype(jnp.float32)
    meansq = lax.optimization_barrier(jnp.mean(wide * wide, axis=-1, keepdims=True))
    return (wide * lax.rsqrt(meansq + 1e-06)).astype(jnp.bfloat16)

def project_spatial(tokens, weight):
    patches, groups, width = tokens.shape
    normed = rms_normalize(tokens).reshape(patches * groups, width)
    stacked = jnp.dot(normed, weight, preferred_element_type=jnp.float32).astype(jnp.bfloat16)
    stacked = stacked.reshape(patches, groups, 3, width).transpose(2, 0, 1, 3)
    return stacked.reshape(3, patches, groups * width)

def pair_attention(operands):
    stacked, keep_row = operands
    query, keyed, valued = (stacked[0], stacked[1], stacked[2])
    scale = query.shape[-1] ** (-0.5)
    scores = jnp.dot(query, keyed.T, preferred_element_type=jnp.float32) * scale
    weights = jnp.exp(scores) * keep_row[None, :]
    probs = (weights / lax.optimization_barrier(jnp.sum(weights, axis=-1, keepdims=True))).astype(jnp.bfloat16)
    return jnp.dot(probs, valued, preferred_element_type=jnp.float32).astype(jnp.bfloat16)

def spatial_attention(stacked, keep_rows):
    three, patches, columns = stacked.shape
    pairs = keep_rows.shape[0]
    split = stacked.reshape(3, patches, pairs, columns // pairs).transpose(2, 0, 1, 3)
    result = lax.map(jax.checkpoint(pair_attention), (split, keep_rows))
    return result.transpose(1, 0, 2).reshape(patches, columns)

def block_group(tokens, attended, w_so, w_gqkv, w_go):
    patches, groups, width = tokens.shape
    rows = patches * groups
    heads = H
    y_first = (tokens.reshape(rows, width).astype(jnp.float32) + jnp.dot(attended.reshape(rows, width), w_so, preferred_element_type=jnp.float32)).astype(jnp.bfloat16)
    normed = rms_normalize(y_first)
    stacked = jnp.dot(normed, w_gqkv, preferred_element_type=jnp.float32).astype(jnp.bfloat16)
    stacked = stacked.reshape(patches, groups, 3, heads, width // heads)
    query = stacked[:, :, 0].astype(jnp.float32)
    keyed = stacked[:, :, 1].astype(jnp.float32)
    valued = stacked[:, :, 2].astype(jnp.float32)
    scale = (width // heads) ** (-0.5)
    scores = jnp.einsum('pgne,pkne->pngk', query, keyed) * scale
    weights = jnp.exp(scores)
    probs = (weights / lax.optimization_barrier(jnp.sum(weights, axis=-1, keepdims=True))).astype(jnp.bfloat16)
    result = jnp.einsum('pngk,pkne->pgne', probs.astype(jnp.float32), valued).astype(jnp.bfloat16)
    result = result.reshape(rows, width)
    mixed = (y_first.astype(jnp.float32) + jnp.dot(result, w_go, preferred_element_type=jnp.float32)).astype(jnp.bfloat16)
    return mixed.reshape(patches, groups, width)

def reference(tokens, cotangent, w_sqkv, w_so, w_gqkv, w_go, keep):
    pair_group = jnp.arange(G * H, dtype=jnp.int32) // H
    keep_rows = keep.astype(jnp.float32)[pair_group]
    stacked, pull_first = jax.vjp(partial(project_spatial, weight=w_sqkv), tokens)
    attended, pull_spatial = jax.vjp(partial(spatial_attention, keep_rows=keep_rows), stacked)
    mixed, pull_group = jax.vjp(partial(block_group, w_so=w_so, w_gqkv=w_gqkv, w_go=w_go), tokens, attended)
    grad_direct, grad_attended = pull_group(cotangent)
    grad_stacked, = pull_spatial(grad_attended)
    grad_first, = pull_first(grad_stacked)
    return (mixed, grad_direct + grad_first)
```

```python
from functools import partial

import jax
import jax.numpy as jnp
from jax import lax
from jax.experimental import pallas as pl
from jax.experimental.pallas import tpu as pltpu
from jax.sharding import PartitionSpec as P

H = 16
G = 32


def rms_normalize(values):
    wide = values.astype(jnp.float32)
    meansq = jnp.mean(wide * wide, axis=-1, keepdims=True)
    return (wide * lax.rsqrt(meansq + 1e-06)).astype(jnp.bfloat16)


def project_spatial(tokens, weight):
    patches, groups, width = tokens.shape
    normed = rms_normalize(tokens).reshape(patches * groups, width)
    stacked = jnp.dot(normed, weight, preferred_element_type=jnp.float32).astype(jnp.bfloat16)
    stacked = stacked.reshape(patches, groups, 3, width).transpose(2, 0, 1, 3)
    return stacked.reshape(3, patches, groups * width)


def pair_attention(operands):
    stacked, keep_row = operands
    query, keyed, valued = (stacked[0], stacked[1], stacked[2])
    scale = query.shape[-1] ** (-0.5)
    scores = jnp.dot(query, keyed.T, preferred_element_type=jnp.float32) * scale
    weights = jnp.exp(scores) * keep_row[None, :]
    probs = (weights / jnp.sum(weights, axis=-1, keepdims=True)).astype(jnp.bfloat16)
    return jnp.dot(probs, valued, preferred_element_type=jnp.float32).astype(jnp.bfloat16)


def spatial_attention(stacked, keep_rows, attend):
    three, patches, columns = stacked.shape
    pairs = keep_rows.shape[0]
    split = stacked.reshape(3, patches, pairs, columns // pairs).transpose(2, 0, 1, 3)
    result = lax.map(attend, (split, keep_rows))
    return result.transpose(1, 0, 2).reshape(patches, columns)


def block_group(tokens, attended, w_so, w_gqkv, w_go):
    patches, groups, width = tokens.shape
    rows = patches * groups
    heads = H
    y_first = (
        tokens.reshape(rows, width).astype(jnp.float32)
        + jnp.dot(attended.reshape(rows, width), w_so, preferred_element_type=jnp.float32)
    ).astype(jnp.bfloat16)
    normed = rms_normalize(y_first)
    stacked = jnp.dot(normed, w_gqkv, preferred_element_type=jnp.float32).astype(jnp.bfloat16)
    stacked = stacked.reshape(patches, groups, 3, heads, width // heads)
    query = stacked[:, :, 0].astype(jnp.float32)
    keyed = stacked[:, :, 1].astype(jnp.float32)
    valued = stacked[:, :, 2].astype(jnp.float32)
    scale = (width // heads) ** (-0.5)
    scores = jnp.einsum("pgne,pkne->pngk", query, keyed) * scale
    weights = jnp.exp(scores)
    probs = (weights / jnp.sum(weights, axis=-1, keepdims=True)).astype(jnp.bfloat16)
    result = jnp.einsum("pngk,pkne->pgne", probs.astype(jnp.float32), valued).astype(jnp.bfloat16)
    result = result.reshape(rows, width)
    mixed = (
        y_first.astype(jnp.float32) + jnp.dot(result, w_go, preferred_element_type=jnp.float32)
    ).astype(jnp.bfloat16)
    return mixed.reshape(patches, groups, width)


def local_any(tokens, cotangent, w_sqkv, w_so, w_gqkv, w_go, keep):
    grid_size = lax.axis_size("grid")
    position = lax.axis_index("grid")
    full_sqkv, full_so, full_gqkv, full_go = (
        lax.all_gather(w_sqkv, "grid", axis=0, tiled=True),
        lax.all_gather(w_so, "grid", axis=0, tiled=True),
        lax.all_gather(w_gqkv, "grid", axis=0, tiled=True),
        lax.all_gather(w_go, "grid", axis=0, tiled=True),
    )
    stacked, pull_first = jax.vjp(partial(project_spatial, weight=full_sqkv), tokens)
    banded = lax.all_to_all(stacked, "grid", split_axis=2, concat_axis=1, tiled=True)
    pairs = G * H // grid_size
    pair_ids = position * pairs + jnp.arange(pairs, dtype=jnp.int32)
    select = (pair_ids[:, None] // H == jnp.arange(G, dtype=jnp.int32)[None, :]).astype(jnp.float32)
    keep_rows = jnp.dot(select, keep.astype(jnp.float32), precision=lax.Precision.HIGHEST)
    attend = jax.checkpoint(pair_attention)
    attended_bands, pull_spatial = jax.vjp(
        partial(spatial_attention, keep_rows=keep_rows, attend=attend), banded
    )
    attended = lax.all_to_all(attended_bands, "grid", split_axis=0, concat_axis=1, tiled=True)
    mixed, pull_group = jax.vjp(
        partial(block_group, w_so=full_so, w_gqkv=full_gqkv, w_go=full_go), tokens, attended
    )
    grad_direct, grad_attended = pull_group(cotangent)
    grad_bands = lax.all_to_all(grad_attended, "grid", split_axis=1, concat_axis=0, tiled=True)
    (grad_banded,) = pull_spatial(grad_bands)
    grad_stacked = lax.all_to_all(grad_banded, "grid", split_axis=1, concat_axis=2, tiled=True)
    (grad_first,) = pull_first(grad_stacked)
    return (mixed, grad_direct + grad_first)


F32 = jnp.float32
BF16 = jnp.bfloat16
LANES = 128
EPS = 1e-06


def nn(a, b):
    return lax.dot_general(a, b, (((1,), (0,)), ((), ())), preferred_element_type=F32)


def nt(a, b):
    return lax.dot_general(a, b, (((1,), (1,)), ((), ())), preferred_element_type=F32)


def tn(a, b):
    return lax.dot_general(a, b, (((0,), (0,)), ((), ())), preferred_element_type=F32)


def rms_parts(wide):
    inv = lax.rsqrt(jnp.mean(wide * wide, axis=-1, keepdims=True) + EPS)
    return inv, (wide * inv).astype(BF16)


def rms_pull(wide, inv, grad):
    inner = jnp.mean(grad * wide, axis=-1, keepdims=True)
    return grad * inv - wide * (inv * inv * inv * inner)


def halves(head):
    lane = lax.broadcasted_iota(jnp.int32, (1, LANES), 1)
    parts = []
    for index in range(LANES // head):
        parts.append((lane // head == index).astype(F32))
    return parts


def merge(selects, parts):
    total = parts[0] * selects[0]
    for select, part in zip(selects[1:], parts[1:]):
        total = total + part * select
    return total.astype(BF16)


def head_probs(query, keyed, select, mask, scale):
    scores = nt(query * select.astype(BF16), keyed) * scale
    weights = jnp.where(mask, jnp.exp(scores), 0.0)
    return weights * (1.0 / jnp.sum(weights, axis=-1, keepdims=True))


def head_pull(probs, query, keyed, valued, grad, select, scale):
    dprobs = nt(grad * select.astype(BF16), valued).astype(BF16).astype(F32)
    inner = jnp.sum(dprobs * probs, axis=-1, keepdims=True)
    dscores = (probs * (dprobs - inner) * scale).astype(BF16)
    return nn(dscores, keyed), tn(dscores, query), tn(probs.astype(BF16), grad)


def columns_of(qkv_ref, width, block):
    at = block * LANES
    return tuple(qkv_ref[:, part * width + at : part * width + at + LANES] for part in range(3))


def spatial_kernel(head, x_ref, w_ref, w_so_ref, keep_ref, qkv_ref, y_ref, att_ref):
    width = x_ref.shape[1]
    _, normed = rms_parts(x_ref[...].astype(F32))
    tile = 512
    for at in range(0, 3 * width, tile):
        qkv_ref[:, at : at + tile] = nn(normed, w_ref[:, at : at + tile]).astype(BF16)
    rows = x_ref.shape[0]
    mask = jnp.broadcast_to(keep_ref[...], (rows, rows)) > 0.0
    selects = halves(head)
    scale = head ** (-0.5)
    for block in range(width // LANES):
        query, keyed, valued = columns_of(qkv_ref, width, block)
        parts = []
        for select in selects:
            probs = head_probs(query, keyed, select, mask, scale)
            parts.append(nn(probs.astype(BF16), valued))
        att_ref[:, block * LANES : (block + 1) * LANES] = merge(selects, parts)
    attended = att_ref[...]
    for at in range(0, width, tile):
        y_ref[:, at : at + tile] = (
            x_ref[:, at : at + tile].astype(F32) + nn(attended, w_so_ref[:, at : at + tile])
        ).astype(BF16)


def spatial_pull_kernel(
    head, dy_ref, x_ref, qkv_ref, keep_ref, w_so_ref, w_ref, out_ref, datt_ref, dqkv_ref
):
    rows, width = x_ref.shape
    dy = dy_ref[...]
    tile = 512
    for at in range(0, width, tile):
        datt_ref[:, at : at + tile] = nt(dy, w_so_ref[at : at + tile, :]).astype(BF16)
    mask = jnp.broadcast_to(keep_ref[...], (rows, rows)) > 0.0
    selects = halves(head)
    scale = head ** (-0.5)
    for block in range(width // LANES):
        query, keyed, valued = columns_of(qkv_ref, width, block)
        at = block * LANES
        grad = datt_ref[:, at : at + LANES]
        pulled = []
        for select in selects:
            probs = head_probs(query, keyed, select, mask, scale)
            pulled.append(head_pull(probs, query, keyed, valued, grad, select, scale))
        for part in range(3):
            dqkv_ref[:, part * width + at : part * width + at + LANES] = merge(
                selects, [pull[part] for pull in pulled]
            )
    wide = x_ref[...].astype(F32)
    inv, _ = rms_parts(wide)
    dqkv = dqkv_ref[...]
    for at in range(0, width, tile):
        datt_ref[:, at : at + tile] = nt(dqkv, w_ref[at : at + tile, :]).astype(BF16)
    first = rms_pull(wide, inv, datt_ref[...].astype(F32)).astype(BF16)
    out_ref[...] = dy + first


def group_kernel(
    head, patches, y_ref, c_ref, w_ref, w_go_ref, mixed_ref, dy_ref, qkv_ref, att_ref, datt_ref
):
    rows, width = y_ref.shape
    groups = rows // patches
    row = lax.broadcasted_iota(jnp.int32, (rows, rows), 0)
    col = lax.broadcasted_iota(jnp.int32, (rows, rows), 1)
    turn = (col == (row % groups) * patches + row // groups).astype(F32).astype(BF16)
    mask = (row // groups) == (col // groups)
    y_first = nn(turn, y_ref[...])
    inv, normed = rms_parts(y_first)
    cot = c_ref[...]
    tile = 512
    for at in range(0, 3 * width, tile):
        qkv_ref[:, at : at + tile] = nn(normed, w_ref[:, at : at + tile]).astype(BF16)
    for at in range(0, width, tile):
        datt_ref[:, at : at + tile] = nt(cot, w_go_ref[at : at + tile, :]).astype(BF16)
    selects = halves(head)
    scale = head ** (-0.5)
    for block in range(width // LANES):
        query, keyed, valued = columns_of(qkv_ref, width, block)
        at = block * LANES
        grad = datt_ref[:, at : at + LANES]
        parts, pulled = [], []
        for select in selects:
            probs = head_probs(query, keyed, select, mask, scale)
            parts.append(nn(probs.astype(BF16), valued))
            pulled.append(head_pull(probs, query, keyed, valued, grad, select, scale))
        att_ref[:, at : at + LANES] = merge(selects, parts)
        for part in range(3):
            qkv_ref[:, part * width + at : part * width + at + LANES] = merge(
                selects, [pull[part] for pull in pulled]
            )
    attended = att_ref[...]
    for at in range(0, width, tile):
        mixed_ref[:, at : at + tile] = (
            y_first[:, at : at + tile] + nn(attended, w_go_ref[:, at : at + tile])
        ).astype(BF16)
    dqkv = qkv_ref[...]
    for at in range(0, width, tile):
        datt_ref[:, at : at + tile] = nt(dqkv, w_ref[at : at + tile, :]).astype(BF16)
    dy = cot + rms_pull(y_first, inv, datt_ref[...].astype(F32)).astype(BF16)
    dy_ref[...] = tn(turn, dy).astype(BF16)


def on_chip(kernel, operands, outs, scratch, flops, moved):
    arrays, specs = [], []
    for operand in operands:
        array, shape, block = operand if isinstance(operand, tuple) else (operand, operand.shape, 0)
        arrays.append(array)
        specs.append(pl.BlockSpec(shape, lambda _, block=block: (0, block), pipeline_mode=pl.Buffered(1)))
    return pl.pallas_call(
        kernel,
        grid=(1,),
        in_specs=specs,
        out_specs=tuple(pl.BlockSpec(shape, lambda _: (0, 0)) for shape in outs),
        out_shape=tuple(jax.ShapeDtypeStruct(shape, BF16) for shape in outs),
        scratch_shapes=[pltpu.VMEM(shape, BF16) for shape in scratch],
        cost_estimate=pl.CostEstimate(flops=flops, bytes_accessed=moved, transcendentals=0),
    )(*arrays)


def gather_weights(shard):
    return lax.all_gather(shard, "grid", axis=0, tiled=True)


def exchange(rows, grid_size):
    total, width = rows.shape
    split = rows.reshape(grid_size, total // grid_size, width)
    return lax.all_to_all(split, "grid", split_axis=0, concat_axis=0, tiled=True).reshape(
        total, width
    )


def local_bands(tokens, cotangent, w_sqkv, w_so, w_gqkv, w_go, keep):
    patches, groups, width = tokens.shape
    grid_size = lax.axis_size("grid")
    rows = patches * groups
    head = width // H
    position = lax.axis_index("grid")
    weights = gather_weights(jnp.concatenate([w_sqkv, w_gqkv, w_so, w_go], axis=1))
    full_sqkv = (weights, (width, 3 * width), 0)
    full_gqkv = (weights, (width, 3 * width), 1)
    full_so = (weights, (width, width), 6)
    full_go = (weights, (width, width), 7)
    keep_row = lax.dynamic_slice_in_dim(keep, position, 1, axis=0).astype(F32)
    weight = width * width
    product = 2 * rows * weight
    wide, flat = (rows, 3 * width), (rows, width)

    x = exchange(tokens.transpose(1, 0, 2).reshape(flat), grid_size)
    qkv, y_first = on_chip(
        partial(spatial_kernel, head),
        (x, full_sqkv, full_so, keep_row),
        (wide, flat),
        (flat,),
        5 * product,
        8 * weight,
    )
    y_local = exchange(y_first, grid_size)
    mixed, dy_local = on_chip(
        partial(group_kernel, head, patches),
        (y_local, cotangent.reshape(flat), full_gqkv, full_go),
        (flat, flat),
        (wide, flat, flat),
        10 * product,
        8 * weight,
    )
    dy = exchange(dy_local, grid_size)
    (grad,) = on_chip(
        partial(spatial_pull_kernel, head),
        (dy, x, qkv, keep_row, full_so, full_sqkv),
        (flat,),
        (flat, wide),
        6 * product,
        8 * weight,
    )
    grad = exchange(grad, grid_size).reshape(groups, patches, width).transpose(1, 0, 2)
    return mixed.reshape(patches, groups, width), grad


def local(tokens, *rest):
    if lax.axis_size("grid") == tokens.shape[1]:
        return local_bands(tokens, *rest)
    return local_any(tokens, *rest)


def solution(mesh):
    placed = (
        P(("parts", "grid"), None, None),
        P(("parts", "grid"), None, None),
        P("grid", None),
        P("grid", None),
        P("grid", None),
        P("grid", None),
        P(None, "parts"),
    )
    return jax.shard_map(
        local,
        mesh=mesh,
        in_specs=placed,
        out_specs=(P(("parts", "grid"), None, None), P(("parts", "grid"), None, None)),
        check_vma=False,
    )
```

```python
from functools import partial

import jax
import jax.numpy as jnp
from jax import lax
from jax.experimental import pallas as pl
from jax.experimental.pallas import tpu as pltpu
from jax.sharding import PartitionSpec as P

H = 16
G = 32


def rms_normalize(values):
    wide = values.astype(jnp.float32)
    meansq = jnp.mean(wide * wide, axis=-1, keepdims=True)
    return (wide * lax.rsqrt(meansq + 1e-06)).astype(jnp.bfloat16)


def project_spatial(tokens, weight):
    patches, groups, width = tokens.shape
    normed = rms_normalize(tokens).reshape(patches * groups, width)
    stacked = jnp.dot(normed, weight, preferred_element_type=jnp.float32).astype(jnp.bfloat16)
    stacked = stacked.reshape(patches, groups, 3, width).transpose(2, 0, 1, 3)
    return stacked.reshape(3, patches, groups * width)


def pair_attention(operands):
    stacked, keep_row = operands
    query, keyed, valued = (stacked[0], stacked[1], stacked[2])
    scale = query.shape[-1] ** (-0.5)
    scores = jnp.dot(query, keyed.T, preferred_element_type=jnp.float32) * scale
    weights = jnp.exp(scores) * keep_row[None, :]
    probs = (weights / jnp.sum(weights, axis=-1, keepdims=True)).astype(jnp.bfloat16)
    return jnp.dot(probs, valued, preferred_element_type=jnp.float32).astype(jnp.bfloat16)


def spatial_attention(stacked, keep_rows, attend):
    three, patches, columns = stacked.shape
    pairs = keep_rows.shape[0]
    split = stacked.reshape(3, patches, pairs, columns // pairs).transpose(2, 0, 1, 3)
    result = lax.map(attend, (split, keep_rows))
    return result.transpose(1, 0, 2).reshape(patches, columns)


def block_group(tokens, attended, w_so, w_gqkv, w_go):
    patches, groups, width = tokens.shape
    rows = patches * groups
    heads = H
    y_first = (
        tokens.reshape(rows, width).astype(jnp.float32)
        + jnp.dot(attended.reshape(rows, width), w_so, preferred_element_type=jnp.float32)
    ).astype(jnp.bfloat16)
    normed = rms_normalize(y_first)
    stacked = jnp.dot(normed, w_gqkv, preferred_element_type=jnp.float32).astype(jnp.bfloat16)
    stacked = stacked.reshape(patches, groups, 3, heads, width // heads)
    query = stacked[:, :, 0].astype(jnp.float32)
    keyed = stacked[:, :, 1].astype(jnp.float32)
    valued = stacked[:, :, 2].astype(jnp.float32)
    scale = (width // heads) ** (-0.5)
    scores = jnp.einsum("pgne,pkne->pngk", query, keyed) * scale
    weights = jnp.exp(scores)
    probs = (weights / jnp.sum(weights, axis=-1, keepdims=True)).astype(jnp.bfloat16)
    result = jnp.einsum("pngk,pkne->pgne", probs.astype(jnp.float32), valued).astype(jnp.bfloat16)
    result = result.reshape(rows, width)
    mixed = (
        y_first.astype(jnp.float32) + jnp.dot(result, w_go, preferred_element_type=jnp.float32)
    ).astype(jnp.bfloat16)
    return mixed.reshape(patches, groups, width)


def local_any(tokens, cotangent, w_sqkv, w_so, w_gqkv, w_go, keep):
    grid_size = lax.axis_size("grid")
    position = lax.axis_index("grid")
    full_sqkv, full_so, full_gqkv, full_go = (
        lax.all_gather(w_sqkv, "grid", axis=0, tiled=True),
        lax.all_gather(w_so, "grid", axis=0, tiled=True),
        lax.all_gather(w_gqkv, "grid", axis=0, tiled=True),
        lax.all_gather(w_go, "grid", axis=0, tiled=True),
    )
    stacked, pull_first = jax.vjp(partial(project_spatial, weight=full_sqkv), tokens)
    banded = lax.all_to_all(stacked, "grid", split_axis=2, concat_axis=1, tiled=True)
    pairs = G * H // grid_size
    pair_ids = position * pairs + jnp.arange(pairs, dtype=jnp.int32)
    select = (pair_ids[:, None] // H == jnp.arange(G, dtype=jnp.int32)[None, :]).astype(jnp.float32)
    keep_rows = jnp.dot(select, keep.astype(jnp.float32), precision=lax.Precision.HIGHEST)
    attend = jax.checkpoint(pair_attention)
    attended_bands, pull_spatial = jax.vjp(
        partial(spatial_attention, keep_rows=keep_rows, attend=attend), banded
    )
    attended = lax.all_to_all(attended_bands, "grid", split_axis=0, concat_axis=1, tiled=True)
    mixed, pull_group = jax.vjp(
        partial(block_group, w_so=full_so, w_gqkv=full_gqkv, w_go=full_go), tokens, attended
    )
    grad_direct, grad_attended = pull_group(cotangent)
    grad_bands = lax.all_to_all(grad_attended, "grid", split_axis=1, concat_axis=0, tiled=True)
    (grad_banded,) = pull_spatial(grad_bands)
    grad_stacked = lax.all_to_all(grad_banded, "grid", split_axis=1, concat_axis=2, tiled=True)
    (grad_first,) = pull_first(grad_stacked)
    return (mixed, grad_direct + grad_first)


F32 = jnp.float32
BF16 = jnp.bfloat16
LANES = 128
EPS = 1e-06


def nn(a, b):
    return lax.dot_general(a, b, (((1,), (0,)), ((), ())), preferred_element_type=F32)


def nt(a, b):
    return lax.dot_general(a, b, (((1,), (1,)), ((), ())), preferred_element_type=F32)


def tn(a, b):
    return lax.dot_general(a, b, (((0,), (0,)), ((), ())), preferred_element_type=F32)


def rms_parts(wide):
    inv = lax.rsqrt(jnp.mean(wide * wide, axis=-1, keepdims=True) + EPS)
    return inv, (wide * inv).astype(BF16)


def rms_pull(wide, inv, grad):
    inner = jnp.mean(grad * wide, axis=-1, keepdims=True)
    return grad * inv - wide * (inv * inv * inv * inner)


def halves(head):
    lane = lax.broadcasted_iota(jnp.int32, (1, LANES), 1)
    parts = []
    for index in range(LANES // head):
        parts.append((lane // head == index).astype(F32))
    return parts


def merge(selects, parts):
    total = parts[0] * selects[0]
    for select, part in zip(selects[1:], parts[1:]):
        total = total + part * select
    return total.astype(BF16)


def head_probs(query, keyed, select, mask, scale):
    scores = nt(query * select.astype(BF16), keyed) * scale
    weights = jnp.where(mask, jnp.exp(scores), 0.0)
    return weights * (1.0 / jnp.sum(weights, axis=-1, keepdims=True))


def head_pull(probs, query, keyed, valued, grad, select, scale):
    dprobs = nt(grad * select.astype(BF16), valued).astype(BF16).astype(F32)
    inner = jnp.sum(dprobs * probs, axis=-1, keepdims=True)
    dscores = (probs * (dprobs - inner) * scale).astype(BF16)
    return nn(dscores, keyed), tn(dscores, query), tn(probs.astype(BF16), grad)


def columns_of(qkv_ref, width, block):
    at = block * LANES
    return tuple(qkv_ref[:, part * width + at : part * width + at + LANES] for part in range(3))


def spatial_kernel(head, x_ref, w_ref, w_so_ref, keep_ref, qkv_ref, y_ref, att_ref):
    width = x_ref.shape[1]
    _, normed = rms_parts(x_ref[...].astype(F32))
    tile = 512
    for at in range(0, 3 * width, tile):
        qkv_ref[:, at : at + tile] = nn(normed, w_ref[:, at : at + tile]).astype(BF16)
    rows = x_ref.shape[0]
    mask = jnp.broadcast_to(keep_ref[...], (rows, rows)) > 0.0
    selects = halves(head)
    scale = head ** (-0.5)
    for block in range(width // LANES):
        query, keyed, valued = columns_of(qkv_ref, width, block)
        parts = []
        for select in selects:
            probs = head_probs(query, keyed, select, mask, scale)
            parts.append(nn(probs.astype(BF16), valued))
        att_ref[:, block * LANES : (block + 1) * LANES] = merge(selects, parts)
    attended = att_ref[...]
    for at in range(0, width, tile):
        y_ref[:, at : at + tile] = (
            x_ref[:, at : at + tile].astype(F32) + nn(attended, w_so_ref[:, at : at + tile])
        ).astype(BF16)


def spatial_pull_kernel(
    head, dy_ref, x_ref, qkv_ref, keep_ref, w_so_ref, w_ref, out_ref, datt_ref, dqkv_ref
):
    rows, width = x_ref.shape
    dy = dy_ref[...]
    tile = 512
    for at in range(0, width, tile):
        datt_ref[:, at : at + tile] = nt(dy, w_so_ref[at : at + tile, :]).astype(BF16)
    mask = jnp.broadcast_to(keep_ref[...], (rows, rows)) > 0.0
    selects = halves(head)
    scale = head ** (-0.5)
    for block in range(width // LANES):
        query, keyed, valued = columns_of(qkv_ref, width, block)
        at = block * LANES
        grad = datt_ref[:, at : at + LANES]
        pulled = []
        for select in selects:
            probs = head_probs(query, keyed, select, mask, scale)
            pulled.append(head_pull(probs, query, keyed, valued, grad, select, scale))
        for part in range(3):
            dqkv_ref[:, part * width + at : part * width + at + LANES] = merge(
                selects, [pull[part] for pull in pulled]
            )
    wide = x_ref[...].astype(F32)
    inv, _ = rms_parts(wide)
    dqkv = dqkv_ref[...]
    for at in range(0, width, tile):
        datt_ref[:, at : at + tile] = nt(dqkv, w_ref[at : at + tile, :]).astype(BF16)
    first = rms_pull(wide, inv, datt_ref[...].astype(F32)).astype(BF16)
    out_ref[...] = dy + first


def group_kernel(
    head, patches, y_ref, c_ref, w_ref, w_go_ref, mixed_ref, dy_ref, qkv_ref, att_ref, datt_ref
):
    rows, width = y_ref.shape
    groups = rows // patches
    row = lax.broadcasted_iota(jnp.int32, (rows, rows), 0)
    col = lax.broadcasted_iota(jnp.int32, (rows, rows), 1)
    turn = (col == (row % groups) * patches + row // groups).astype(F32).astype(BF16)
    mask = (row // groups) == (col // groups)
    y_first = nn(turn, y_ref[...])
    inv, normed = rms_parts(y_first)
    cot = c_ref[...]
    tile = 512
    for at in range(0, 3 * width, tile):
        qkv_ref[:, at : at + tile] = nn(normed, w_ref[:, at : at + tile]).astype(BF16)
    for at in range(0, width, tile):
        datt_ref[:, at : at + tile] = nt(cot, w_go_ref[at : at + tile, :]).astype(BF16)
    selects = halves(head)
    scale = head ** (-0.5)
    for block in range(width // LANES):
        query, keyed, valued = columns_of(qkv_ref, width, block)
        at = block * LANES
        grad = datt_ref[:, at : at + LANES]
        parts, pulled = [], []
        for select in selects:
            probs = head_probs(query, keyed, select, mask, scale)
            parts.append(nn(probs.astype(BF16), valued))
            pulled.append(head_pull(probs, query, keyed, valued, grad, select, scale))
        att_ref[:, at : at + LANES] = merge(selects, parts)
        for part in range(3):
            qkv_ref[:, part * width + at : part * width + at + LANES] = merge(
                selects, [pull[part] for pull in pulled]
            )
    attended = att_ref[...]
    for at in range(0, width, tile):
        mixed_ref[:, at : at + tile] = (
            y_first[:, at : at + tile] + nn(attended, w_go_ref[:, at : at + tile])
        ).astype(BF16)
    dqkv = qkv_ref[...]
    for at in range(0, width, tile):
        datt_ref[:, at : at + tile] = nt(dqkv, w_ref[at : at + tile, :]).astype(BF16)
    dy = cot + rms_pull(y_first, inv, datt_ref[...].astype(F32)).astype(BF16)
    dy_ref[...] = tn(turn, dy).astype(BF16)


def on_chip(kernel, operands, outs, scratch, flops, moved):
    arrays, specs = [], []
    for operand in operands:
        array, shape, block = operand if isinstance(operand, tuple) else (operand, operand.shape, (0,) * operand.ndim)
        arrays.append(array)
        specs.append(pl.BlockSpec(shape, lambda _, block=block: block, pipeline_mode=pl.Buffered(1)))
    return pl.pallas_call(
        kernel,
        grid=(1,),
        in_specs=specs,
        out_specs=tuple(pl.BlockSpec(shape, lambda _: (0, 0)) for shape in outs),
        out_shape=tuple(jax.ShapeDtypeStruct(shape, BF16) for shape in outs),
        scratch_shapes=[pltpu.VMEM(shape, BF16) for shape in scratch],
        cost_estimate=pl.CostEstimate(flops=flops, bytes_accessed=moved, transcendentals=0),
    )(*arrays)


SPLIT = (2, 2, 2)


def gather_kernel(shard_ref, full_ref, send_sem, recv_sem, own_sem):
    count = lax.axis_size("grid")
    ny, nx, nc = SPLIT
    depth = count // (ny * nx * nc)
    part = lax.axis_index("parts")
    me = lax.axis_index("grid")
    core, x, y, z = me % 2, (me // 2) % 2, (me // 4) % 2, me // 8
    rows = shard_ref.shape[1]

    def place(z, y, x, core):
        return ((z * ny + y) * nx + x) * nc + core

    def back(k):
        return (z + depth - k) % depth

    zs = [place((z + k) % depth, y, x, core) for k in range(depth)]
    xp, yp, cp = place(z, y, 1 - x, core), place(z, 1 - y, x, core), place(z, y, x, 1 - core)
    peers = zs[1:] + [xp, yp, cp]
    barrier = pltpu.get_barrier_semaphore()
    for peer in peers:
        pl.semaphore_signal(
            barrier, inc=1, device_id=(part, peer), device_id_type=pl.DeviceIdType.MESH
        )
    pl.semaphore_wait(barrier, len(peers))

    slots, sent = {}, []

    def slot(name):
        return slots.setdefault(name, len(slots))

    def region(half, owner):
        return full_ref.at[half, pl.ds(pl.multiple_of(owner * rows, rows), rows), :]

    def copy(name, half, owner, peer, source=None):
        at = slot(name)
        return pltpu.make_async_remote_copy(
            src_ref=region(half, owner) if source is None else source,
            dst_ref=region(half, owner),
            send_sem=send_sem.at[at],
            recv_sem=recv_sem.at[at],
            device_id=(part, peer),
            device_id_type=pl.DeviceIdType.MESH,
        )

    def send(name, half, owner, peer):
        source = shard_ref.at[half] if name[1] == "own" else None
        made = copy(name, half, owner, peer, source)
        made.start()
        sent.append(made)

    def arrive(name, half, owner):
        copy(name, half, owner, me).wait_recv()

    keeps = []
    for half in range(2):
        for k in range(1, depth):
            send(("z", "own", half, k), half, me, zs[k])
    for half in range(2):
        keep = pltpu.make_async_copy(shard_ref.at[half], region(half, me), own_sem.at[half])
        keep.start()
        keeps.append(keep)
    order = ((("y", yp), ("x", xp)), (("x", xp), ("y", yp)))

    def owner_of(half, k, first, second):
        cross_y, cross_x = (first, second) if half == 0 else (second, first)
        return place(back(k), 1 - y if cross_y else y, 1 - x if cross_x else x, core)

    def spread_line(k):
        tag = "own" if k == 0 else "line"
        for half in range(2):
            mine = owner_of(half, k, False, False)
            send(("first", tag, half, k), half, mine, order[half][0][1])
        for half in range(2):
            mine = owner_of(half, k, False, False)
            send(("second", tag, half, k, 0), half, mine, order[half][1][1])
            send(("core", tag, half, k, 0, 0), half, mine, cp)

    def spread_first(k):
        tag = "own" if k == 0 else "line"
        for half in range(2):
            got = owner_of(half, k, True, False)
            arrive(("first", tag, half, k), half, got)
            send(("second", "far", half, k, 1), half, got, order[half][1][1])
            send(("core", "far", half, k, 1, 0), half, got, cp)

    def spread_second(k, first):
        tag = "far" if first else ("own" if k == 0 else "line")
        for half in range(2):
            got = owner_of(half, k, bool(first), True)
            arrive(("second", tag, half, k, first), half, got)
            send(("core", "far", half, k, first, 1), half, got, cp)

    spread_line(0)
    for k in range(1, depth):
        for half in range(2):
            arrive(("z", "own", half, k), half, place(back(k), y, x, core))
        spread_line(k)
        spread_first(k - 1)
        spread_second(k - 1, 0)
    spread_first(depth - 1)
    for k in range(depth - 1):
        spread_second(k, 1)
    spread_second(depth - 1, 0)
    spread_second(depth - 1, 1)
    for k in range(depth):
        for first in range(2):
            for second in range(2):
                tag = "far" if first or second else ("own" if k == 0 else "line")
                for half in range(2):
                    cross_y, cross_x = (first, second) if half == 0 else (second, first)
                    got = place(
                        back(k), 1 - y if cross_y else y, 1 - x if cross_x else x, 1 - core
                    )
                    arrive(("core", tag, half, k, first, second), half, got)
    for made in sent:
        made.wait_send()
    for keep in keeps:
        keep.wait()


def gather_weights(shard):
    halves_, rows, columns = shard.shape
    count = lax.axis_size("grid")
    transfers = 2 * (count // 8 - 1) + 8 * (count // 8) + 4 * (count // 8)
    transfers += 2 * (count // 8)
    return pl.pallas_call(
        gather_kernel,
        in_specs=[pl.BlockSpec(memory_space=pltpu.VMEM)],
        out_specs=pl.BlockSpec(memory_space=pl.ANY),
        out_shape=jax.ShapeDtypeStruct((halves_, rows * count, columns), BF16),
        scratch_shapes=[
            pltpu.SemaphoreType.DMA((transfers,)),
            pltpu.SemaphoreType.DMA((transfers,)),
            pltpu.SemaphoreType.DMA((2,)),
        ],
        compiler_params=pltpu.CompilerParams(collective_id=0, has_side_effects=True),
    )(shard)


def exchange(rows, grid_size):
    total, width = rows.shape
    split = rows.reshape(grid_size, total // grid_size, width)
    return lax.all_to_all(split, "grid", split_axis=0, concat_axis=0, tiled=True).reshape(
        total, width
    )


def local_bands(tokens, cotangent, w_sqkv, w_so, w_gqkv, w_go, keep):
    patches, groups, width = tokens.shape
    grid_size = lax.axis_size("grid")
    rows = patches * groups
    head = width // H
    position = lax.axis_index("grid")
    shards = [jnp.concatenate(pair, axis=1) for pair in ((w_sqkv, w_so), (w_gqkv, w_go))]
    weights = gather_weights(jnp.stack(shards))
    full_sqkv = (weights, (None, width, 3 * width), (0, 0, 0))
    full_so = (weights, (None, width, width), (0, 0, 3))
    full_gqkv = (weights, (None, width, 3 * width), (1, 0, 0))
    full_go = (weights, (None, width, width), (1, 0, 3))
    keep_row = lax.dynamic_slice_in_dim(keep, position, 1, axis=0).astype(F32)
    weight = width * width
    product = 2 * rows * weight
    wide, flat = (rows, 3 * width), (rows, width)

    x = exchange(tokens.transpose(1, 0, 2).reshape(flat), grid_size)
    qkv, y_first = on_chip(
        partial(spatial_kernel, head),
        (x, full_sqkv, full_so, keep_row),
        (wide, flat),
        (flat,),
        5 * product,
        8 * weight,
    )
    y_local = exchange(y_first, grid_size)
    mixed, dy_local = on_chip(
        partial(group_kernel, head, patches),
        (y_local, cotangent.reshape(flat), full_gqkv, full_go),
        (flat, flat),
        (wide, flat, flat),
        10 * product,
        8 * weight,
    )
    dy = exchange(dy_local, grid_size)
    (grad,) = on_chip(
        partial(spatial_pull_kernel, head),
        (dy, x, qkv, keep_row, full_so, full_sqkv),
        (flat,),
        (flat, wide),
        6 * product,
        8 * weight,
    )
    grad = exchange(grad, grid_size).reshape(groups, patches, width).transpose(1, 0, 2)
    return mixed.reshape(patches, groups, width), grad


def local(tokens, *rest):
    if lax.axis_size("grid") == tokens.shape[1]:
        return local_bands(tokens, *rest)
    return local_any(tokens, *rest)


def solution(mesh):
    placed = (
        P(("parts", "grid"), None, None),
        P(("parts", "grid"), None, None),
        P("grid", None),
        P("grid", None),
        P("grid", None),
        P("grid", None),
        P(None, "parts"),
    )
    return jax.shard_map(
        local,
        mesh=mesh,
        in_specs=placed,
        out_specs=(P(("parts", "grid"), None, None), P(("parts", "grid"), None, None)),
        check_vma=False,
    )
```

```python
from functools import partial

import jax
import jax.numpy as jnp
from jax import lax
from jax.experimental import pallas as pl
from jax.experimental.pallas import tpu as pltpu
from jax.sharding import PartitionSpec as P

H = 16
G = 32


def rms_normalize(values):
    wide = values.astype(jnp.float32)
    meansq = jnp.mean(wide * wide, axis=-1, keepdims=True)
    return (wide * lax.rsqrt(meansq + 1e-06)).astype(jnp.bfloat16)


def project_spatial(tokens, weight):
    patches, groups, width = tokens.shape
    normed = rms_normalize(tokens).reshape(patches * groups, width)
    stacked = jnp.dot(normed, weight, preferred_element_type=jnp.float32).astype(jnp.bfloat16)
    stacked = stacked.reshape(patches, groups, 3, width).transpose(2, 0, 1, 3)
    return stacked.reshape(3, patches, groups * width)


def pair_attention(operands):
    stacked, keep_row = operands
    query, keyed, valued = (stacked[0], stacked[1], stacked[2])
    scale = query.shape[-1] ** (-0.5)
    scores = jnp.dot(query, keyed.T, preferred_element_type=jnp.float32) * scale
    weights = jnp.exp(scores) * keep_row[None, :]
    probs = (weights / jnp.sum(weights, axis=-1, keepdims=True)).astype(jnp.bfloat16)
    return jnp.dot(probs, valued, preferred_element_type=jnp.float32).astype(jnp.bfloat16)


def spatial_attention(stacked, keep_rows, attend):
    three, patches, columns = stacked.shape
    pairs = keep_rows.shape[0]
    split = stacked.reshape(3, patches, pairs, columns // pairs).transpose(2, 0, 1, 3)
    result = lax.map(attend, (split, keep_rows))
    return result.transpose(1, 0, 2).reshape(patches, columns)


def block_group(tokens, attended, w_so, w_gqkv, w_go):
    patches, groups, width = tokens.shape
    rows = patches * groups
    heads = H
    y_first = (
        tokens.reshape(rows, width).astype(jnp.float32)
        + jnp.dot(attended.reshape(rows, width), w_so, preferred_element_type=jnp.float32)
    ).astype(jnp.bfloat16)
    normed = rms_normalize(y_first)
    stacked = jnp.dot(normed, w_gqkv, preferred_element_type=jnp.float32).astype(jnp.bfloat16)
    stacked = stacked.reshape(patches, groups, 3, heads, width // heads)
    query = stacked[:, :, 0].astype(jnp.float32)
    keyed = stacked[:, :, 1].astype(jnp.float32)
    valued = stacked[:, :, 2].astype(jnp.float32)
    scale = (width // heads) ** (-0.5)
    scores = jnp.einsum("pgne,pkne->pngk", query, keyed) * scale
    weights = jnp.exp(scores)
    probs = (weights / jnp.sum(weights, axis=-1, keepdims=True)).astype(jnp.bfloat16)
    result = jnp.einsum("pngk,pkne->pgne", probs.astype(jnp.float32), valued).astype(jnp.bfloat16)
    result = result.reshape(rows, width)
    mixed = (
        y_first.astype(jnp.float32) + jnp.dot(result, w_go, preferred_element_type=jnp.float32)
    ).astype(jnp.bfloat16)
    return mixed.reshape(patches, groups, width)


def local_any(tokens, cotangent, w_sqkv, w_so, w_gqkv, w_go, keep):
    grid_size = lax.axis_size("grid")
    position = lax.axis_index("grid")
    full_sqkv, full_so, full_gqkv, full_go = (
        lax.all_gather(w_sqkv, "grid", axis=0, tiled=True),
        lax.all_gather(w_so, "grid", axis=0, tiled=True),
        lax.all_gather(w_gqkv, "grid", axis=0, tiled=True),
        lax.all_gather(w_go, "grid", axis=0, tiled=True),
    )
    stacked, pull_first = jax.vjp(partial(project_spatial, weight=full_sqkv), tokens)
    banded = lax.all_to_all(stacked, "grid", split_axis=2, concat_axis=1, tiled=True)
    pairs = G * H // grid_size
    pair_ids = position * pairs + jnp.arange(pairs, dtype=jnp.int32)
    select = (pair_ids[:, None] // H == jnp.arange(G, dtype=jnp.int32)[None, :]).astype(jnp.float32)
    keep_rows = jnp.dot(select, keep.astype(jnp.float32), precision=lax.Precision.HIGHEST)
    attend = jax.checkpoint(pair_attention)
    attended_bands, pull_spatial = jax.vjp(
        partial(spatial_attention, keep_rows=keep_rows, attend=attend), banded
    )
    attended = lax.all_to_all(attended_bands, "grid", split_axis=0, concat_axis=1, tiled=True)
    mixed, pull_group = jax.vjp(
        partial(block_group, w_so=full_so, w_gqkv=full_gqkv, w_go=full_go), tokens, attended
    )
    grad_direct, grad_attended = pull_group(cotangent)
    grad_bands = lax.all_to_all(grad_attended, "grid", split_axis=1, concat_axis=0, tiled=True)
    (grad_banded,) = pull_spatial(grad_bands)
    grad_stacked = lax.all_to_all(grad_banded, "grid", split_axis=1, concat_axis=2, tiled=True)
    (grad_first,) = pull_first(grad_stacked)
    return (mixed, grad_direct + grad_first)


F32 = jnp.float32
BF16 = jnp.bfloat16
LANES = 128
EPS = 1e-06


def nn(a, b):
    return lax.dot_general(a, b, (((1,), (0,)), ((), ())), preferred_element_type=F32)


def nt(a, b):
    return lax.dot_general(a, b, (((1,), (1,)), ((), ())), preferred_element_type=F32)


def tn(a, b):
    return lax.dot_general(a, b, (((0,), (0,)), ((), ())), preferred_element_type=F32)


def rms_parts(wide):
    inv = lax.rsqrt(jnp.mean(wide * wide, axis=-1, keepdims=True) + EPS)
    return inv, (wide * inv).astype(BF16)


def rms_pull(wide, inv, grad):
    inner = jnp.mean(grad * wide, axis=-1, keepdims=True)
    return grad * inv - wide * (inv * inv * inv * inner)


def halves(head):
    lane = lax.broadcasted_iota(jnp.int32, (1, LANES), 1)
    parts = []
    for index in range(LANES // head):
        parts.append((lane // head == index).astype(F32))
    return parts


def merge(selects, parts):
    total = parts[0] * selects[0]
    for select, part in zip(selects[1:], parts[1:]):
        total = total + part * select
    return total.astype(BF16)


def head_probs(query, keyed, select, mask, scale):
    scores = nt(query * select.astype(BF16), keyed) * scale
    weights = jnp.where(mask, jnp.exp(scores), 0.0)
    return weights * (1.0 / jnp.sum(weights, axis=-1, keepdims=True))


def head_pull(probs, query, keyed, valued, grad, select, scale):
    dprobs = nt(grad * select.astype(BF16), valued).astype(BF16).astype(F32)
    inner = jnp.sum(dprobs * probs, axis=-1, keepdims=True)
    dscores = (probs * (dprobs - inner) * scale).astype(BF16)
    return nn(dscores, keyed), tn(dscores, query), tn(probs.astype(BF16), grad)


def columns_of(qkv_ref, width, block):
    at = block * LANES
    return tuple(qkv_ref[:, part * width + at : part * width + at + LANES] for part in range(3))


def spatial_kernel(head, x_ref, w_ref, w_so_ref, keep_ref, qkv_ref, y_ref, att_ref):
    width = x_ref.shape[1]
    _, normed = rms_parts(x_ref[...].astype(F32))
    tile = 512
    for at in range(0, 3 * width, tile):
        qkv_ref[:, at : at + tile] = nn(normed, w_ref[:, at : at + tile]).astype(BF16)
    rows = x_ref.shape[0]
    mask = jnp.broadcast_to(keep_ref[...], (rows, rows)) > 0.0
    selects = halves(head)
    scale = head ** (-0.5)
    for block in range(width // LANES):
        query, keyed, valued = columns_of(qkv_ref, width, block)
        parts = []
        for select in selects:
            probs = head_probs(query, keyed, select, mask, scale)
            parts.append(nn(probs.astype(BF16), valued))
        att_ref[:, block * LANES : (block + 1) * LANES] = merge(selects, parts)
    attended = att_ref[...]
    for at in range(0, width, tile):
        y_ref[:, at : at + tile] = (
            x_ref[:, at : at + tile].astype(F32) + nn(attended, w_so_ref[:, at : at + tile])
        ).astype(BF16)


def spatial_pull_kernel(
    head, dy_ref, x_ref, qkv_ref, keep_ref, w_so_ref, w_ref, out_ref, datt_ref, dqkv_ref
):
    rows, width = x_ref.shape
    dy = dy_ref[...]
    tile = 512
    for at in range(0, width, tile):
        datt_ref[:, at : at + tile] = nt(dy, w_so_ref[at : at + tile, :]).astype(BF16)
    mask = jnp.broadcast_to(keep_ref[...], (rows, rows)) > 0.0
    selects = halves(head)
    scale = head ** (-0.5)
    for block in range(width // LANES):
        query, keyed, valued = columns_of(qkv_ref, width, block)
        at = block * LANES
        grad = datt_ref[:, at : at + LANES]
        pulled = []
        for select in selects:
            probs = head_probs(query, keyed, select, mask, scale)
            pulled.append(head_pull(probs, query, keyed, valued, grad, select, scale))
        for part in range(3):
            dqkv_ref[:, part * width + at : part * width + at + LANES] = merge(
                selects, [pull[part] for pull in pulled]
            )
    wide = x_ref[...].astype(F32)
    inv, _ = rms_parts(wide)
    dqkv = dqkv_ref[...]
    for at in range(0, width, tile):
        datt_ref[:, at : at + tile] = nt(dqkv, w_ref[at : at + tile, :]).astype(BF16)
    first = rms_pull(wide, inv, datt_ref[...].astype(F32)).astype(BF16)
    out_ref[...] = dy + first


def group_kernel(
    head, patches, y_ref, c_ref, w_ref, w_go_ref, mixed_ref, dy_ref, qkv_ref, att_ref, datt_ref
):
    rows, width = y_ref.shape
    groups = rows // patches
    row = lax.broadcasted_iota(jnp.int32, (rows, rows), 0)
    col = lax.broadcasted_iota(jnp.int32, (rows, rows), 1)
    turn = (col == (row % groups) * patches + row // groups).astype(F32).astype(BF16)
    mask = (row // groups) == (col // groups)
    y_first = nn(turn, y_ref[...])
    inv, normed = rms_parts(y_first)
    cot = c_ref[...]
    tile = 512
    for at in range(0, 3 * width, tile):
        qkv_ref[:, at : at + tile] = nn(normed, w_ref[:, at : at + tile]).astype(BF16)
    for at in range(0, width, tile):
        datt_ref[:, at : at + tile] = nt(cot, w_go_ref[at : at + tile, :]).astype(BF16)
    selects = halves(head)
    scale = head ** (-0.5)
    for block in range(width // LANES):
        query, keyed, valued = columns_of(qkv_ref, width, block)
        at = block * LANES
        grad = datt_ref[:, at : at + LANES]
        parts, pulled = [], []
        for select in selects:
            probs = head_probs(query, keyed, select, mask, scale)
            parts.append(nn(probs.astype(BF16), valued))
            pulled.append(head_pull(probs, query, keyed, valued, grad, select, scale))
        att_ref[:, at : at + LANES] = merge(selects, parts)
        for part in range(3):
            qkv_ref[:, part * width + at : part * width + at + LANES] = merge(
                selects, [pull[part] for pull in pulled]
            )
    attended = att_ref[...]
    for at in range(0, width, tile):
        mixed_ref[:, at : at + tile] = (
            y_first[:, at : at + tile] + nn(attended, w_go_ref[:, at : at + tile])
        ).astype(BF16)
    dqkv = qkv_ref[...]
    for at in range(0, width, tile):
        datt_ref[:, at : at + tile] = nt(dqkv, w_ref[at : at + tile, :]).astype(BF16)
    dy = cot + rms_pull(y_first, inv, datt_ref[...].astype(F32)).astype(BF16)
    dy_ref[...] = tn(turn, dy).astype(BF16)


def on_chip(kernel, operands, outs, scratch, flops, moved):
    arrays, specs = [], []
    for operand in operands:
        array, shape, block = operand if isinstance(operand, tuple) else (operand, operand.shape, (0,) * operand.ndim)
        arrays.append(array)
        specs.append(pl.BlockSpec(shape, lambda _, block=block: block, pipeline_mode=pl.Buffered(1)))
    return pl.pallas_call(
        kernel,
        grid=(1,),
        in_specs=specs,
        out_specs=tuple(pl.BlockSpec(shape, lambda _: (0, 0)) for shape in outs),
        out_shape=tuple(jax.ShapeDtypeStruct(shape, BF16) for shape in outs),
        scratch_shapes=[pltpu.VMEM(shape, BF16) for shape in scratch],
        cost_estimate=pl.CostEstimate(flops=flops, bytes_accessed=moved, transcendentals=0),
    )(*arrays)


SPLIT = (2, 2, 2)


def gather_kernel(shard_ref, full_ref, send_sem, recv_sem, own_sem):
    count = lax.axis_size("grid")
    ny, nx, nc = SPLIT
    depth = count // (ny * nx * nc)
    part = lax.axis_index("parts")
    me = lax.axis_index("grid")
    core, x, y, z = me % 2, (me // 2) % 2, (me // 4) % 2, me // 8
    rows, columns = shard_ref.shape
    cuts = part_cuts(columns)

    def place(z, y, x, core):
        return ((z * ny + y) * nx + x) * nc + core

    def back(k):
        return (z + depth - k) % depth

    zs = [place((z + k) % depth, y, x, core) for k in range(depth)]
    xp, yp, cp = place(z, y, 1 - x, core), place(z, 1 - y, x, core), place(z, y, x, 1 - core)
    peers = zs[1:] + [xp, yp, cp]
    barrier = pltpu.get_barrier_semaphore()
    for peer in peers:
        pl.semaphore_signal(
            barrier, inc=1, device_id=(part, peer), device_id_type=pl.DeviceIdType.MESH
        )
    pl.semaphore_wait(barrier, len(peers))

    slots, sent = {}, []

    def slot(name):
        return slots.setdefault(name, len(slots))

    def region(half, owner):
        low, high = cuts[half]
        return full_ref.at[pl.ds(pl.multiple_of(owner * rows, rows), rows), low:high]

    def own(half):
        low, high = cuts[half]
        return shard_ref.at[:, low:high]

    def copy(name, half, owner, peer, source=None):
        at = slot(name)
        return pltpu.make_async_remote_copy(
            src_ref=region(half, owner) if source is None else source,
            dst_ref=region(half, owner),
            send_sem=send_sem.at[at],
            recv_sem=recv_sem.at[at],
            device_id=(part, peer),
            device_id_type=pl.DeviceIdType.MESH,
        )

    def send(name, half, owner, peer):
        source = own(half) if name[1] == "own" else None
        made = copy(name, half, owner, peer, source)
        made.start()
        sent.append(made)

    def arrive(name, half, owner):
        copy(name, half, owner, me).wait_recv()

    send(("cx", "own"), 2, me, xp)
    for k in range(1, depth):
        for half in range(2):
            send(("z", "own", half, k), half, me, zs[k])
    keep = pltpu.make_async_copy(shard_ref, full_ref.at[pl.ds(pl.multiple_of(me * rows, rows), rows), :], own_sem)
    keep.start()
    order = ((("y", yp), ("x", xp)), (("x", xp), ("y", yp)))

    def owner_of(half, k, first, second):
        cross_y, cross_x = (first, second) if half == 0 else (second, first)
        return place(back(k), 1 - y if cross_y else y, 1 - x if cross_x else x, core)

    def spread_line(k):
        tag = "own" if k == 0 else "line"
        for half in range(2):
            mine = owner_of(half, k, False, False)
            send(("first", tag, half, k), half, mine, order[half][0][1])
        for half in range(2):
            mine = owner_of(half, k, False, False)
            send(("second", tag, half, k, 0), half, mine, order[half][1][1])
            send(("core", tag, half, k, 0, 0), half, mine, cp)

    def spread_first(k):
        tag = "own" if k == 0 else "line"
        for half in range(2):
            got = owner_of(half, k, True, False)
            arrive(("first", tag, half, k), half, got)
            send(("second", "far", half, k, 1), half, got, order[half][1][1])
            send(("core", "far", half, k, 1, 0), half, got, cp)

    def spread_second(k, first):
        tag = "far" if first else ("own" if k == 0 else "line")
        for half in range(2):
            got = owner_of(half, k, bool(first), True)
            arrive(("second", tag, half, k, first), half, got)
            send(("core", "far", half, k, first, 1), half, got, cp)

    across = place(z, y, 1 - x, core)
    spread_line(0)
    send(("cy", "own", 0), 2, me, yp)
    send(("ccore", "own", 0, 0, 0), 2, me, cp)
    for k in range(1, depth):
        send(("cz", "own", k, 0, 0), 2, me, zs[k])
    arrive(("cx", "own"), 2, across)
    send(("cy", "far", 1), 2, across, yp)
    send(("ccore", "far", 0, 0, 1), 2, across, cp)
    for k in range(1, depth):
        send(("cz", "far", k, 0, 1), 2, across, zs[k])
    spread_first(0)
    for cross in range(2):
        got = place(z, 1 - y, 1 - x if cross else x, core)
        arrive(("cy", "far" if cross else "own", cross), 2, got)
        send(("ccore", "far", 0, 1, cross), 2, got, cp)
        for k in range(1, depth):
            send(("cz", "far", k, 1, cross), 2, got, zs[k])
    for k in range(1, depth):
        for half in range(2):
            arrive(("z", "own", half, k), half, place(back(k), y, x, core))
        spread_line(k)
        spread_second(k - 1, 0)
        if k > 1:
            spread_second(k - 2, 1)
        spread_first(k)
    spread_second(depth - 2, 1)
    spread_second(depth - 1, 0)
    for k in range(1, depth):
        for cross_y in range(2):
            for cross_x in range(2):
                tag = "far" if cross_y or cross_x else "own"
                got = place(back(k), 1 - y if cross_y else y, 1 - x if cross_x else x, core)
                arrive(("cz", tag, k, cross_y, cross_x), 2, got)
                send(("ccore", "far", k, cross_y, cross_x), 2, got, cp)
    spread_second(depth - 1, 1)
    for k in range(depth):
        for first in range(2):
            for second in range(2):
                tag = "far" if first or second else ("own" if k == 0 else "line")
                for half in range(2):
                    cross_y, cross_x = (first, second) if half == 0 else (second, first)
                    got = place(
                        back(k), 1 - y if cross_y else y, 1 - x if cross_x else x, 1 - core
                    )
                    arrive(("core", tag, half, k, first, second), half, got)
                got = place(back(k), 1 - y if first else y, 1 - x if second else x, 1 - core)
                tag = "far" if first or second or k else "own"
                arrive(("ccore", tag, k, first, second), 2, got)
    for made in sent:
        made.wait_send()
    keep.wait()


def part_cuts(columns):
    unit = columns // 32
    return ((0, 13 * unit), (13 * unit, 26 * unit), (26 * unit, columns))


def gather_weights(shard):
    rows, columns = shard.shape
    count = lax.axis_size("grid")
    depth = count // 8
    transfers = (2 * (depth - 1) + 14 * depth) + (3 + 4 * (depth - 1) + 4 * depth)
    return pl.pallas_call(
        gather_kernel,
        in_specs=[pl.BlockSpec(memory_space=pltpu.VMEM)],
        out_specs=pl.BlockSpec(memory_space=pl.ANY),
        out_shape=jax.ShapeDtypeStruct((rows * count, columns), BF16),
        scratch_shapes=[
            pltpu.SemaphoreType.DMA((transfers,)),
            pltpu.SemaphoreType.DMA((transfers,)),
            pltpu.SemaphoreType.DMA,
        ],
        compiler_params=pltpu.CompilerParams(collective_id=0, has_side_effects=True),
    )(shard)


def exchange(rows, grid_size):
    total, width = rows.shape
    split = rows.reshape(grid_size, total // grid_size, width)
    return lax.all_to_all(split, "grid", split_axis=0, concat_axis=0, tiled=True).reshape(
        total, width
    )


def local_bands(tokens, cotangent, w_sqkv, w_so, w_gqkv, w_go, keep):
    patches, groups, width = tokens.shape
    grid_size = lax.axis_size("grid")
    rows = patches * groups
    head = width // H
    position = lax.axis_index("grid")
    second = lax.all_gather(jnp.concatenate([w_gqkv, w_go], axis=1), "grid", axis=0, tiled=True)
    first = gather_weights(jnp.concatenate([w_sqkv, w_so], axis=1))
    full_sqkv = (first, (width, 3 * width), (0, 0))
    full_so = (first, (width, width), (0, 3))
    full_gqkv = (second, (width, 3 * width), (0, 0))
    full_go = (second, (width, width), (0, 3))
    keep_row = lax.dynamic_slice_in_dim(keep, position, 1, axis=0).astype(F32)
    weight = width * width
    product = 2 * rows * weight
    wide, flat = (rows, 3 * width), (rows, width)

    x = exchange(tokens.transpose(1, 0, 2).reshape(flat), grid_size)
    qkv, y_first = on_chip(
        partial(spatial_kernel, head),
        (x, full_sqkv, full_so, keep_row),
        (wide, flat),
        (flat,),
        5 * product,
        8 * weight,
    )
    y_local = exchange(y_first, grid_size)
    mixed, dy_local = on_chip(
        partial(group_kernel, head, patches),
        (y_local, cotangent.reshape(flat), full_gqkv, full_go),
        (flat, flat),
        (wide, flat, flat),
        10 * product,
        8 * weight,
    )
    dy = exchange(dy_local, grid_size)
    (grad,) = on_chip(
        partial(spatial_pull_kernel, head),
        (dy, x, qkv, keep_row, full_so, full_sqkv),
        (flat,),
        (flat, wide),
        6 * product,
        8 * weight,
    )
    grad = exchange(grad, grid_size).reshape(groups, patches, width).transpose(1, 0, 2)
    return mixed.reshape(patches, groups, width), grad


def local(tokens, *rest):
    if lax.axis_size("grid") == tokens.shape[1]:
        return local_bands(tokens, *rest)
    return local_any(tokens, *rest)


def solution(mesh):
    placed = (
        P(("parts", "grid"), None, None),
        P(("parts", "grid"), None, None),
        P("grid", None),
        P("grid", None),
        P("grid", None),
        P("grid", None),
        P(None, "parts"),
    )
    return jax.shard_map(
        local,
        mesh=mesh,
        in_specs=placed,
        out_specs=(P(("parts", "grid"), None, None), P(("parts", "grid"), None, None)),
        check_vma=False,
    )
```

```python
from functools import partial

import jax
import jax.numpy as jnp
from jax import lax
from jax.experimental import pallas as pl
from jax.experimental.pallas import tpu as pltpu
from jax.sharding import PartitionSpec as P

H = 16
G = 32


def rms_normalize(values):
    wide = values.astype(jnp.float32)
    meansq = jnp.mean(wide * wide, axis=-1, keepdims=True)
    return (wide * lax.rsqrt(meansq + 1e-06)).astype(jnp.bfloat16)


def project_spatial(tokens, weight):
    patches, groups, width = tokens.shape
    normed = rms_normalize(tokens).reshape(patches * groups, width)
    stacked = jnp.dot(normed, weight, preferred_element_type=jnp.float32).astype(jnp.bfloat16)
    stacked = stacked.reshape(patches, groups, 3, width).transpose(2, 0, 1, 3)
    return stacked.reshape(3, patches, groups * width)


def pair_attention(operands):
    stacked, keep_row = operands
    query, keyed, valued = (stacked[0], stacked[1], stacked[2])
    scale = query.shape[-1] ** (-0.5)
    scores = jnp.dot(query, keyed.T, preferred_element_type=jnp.float32) * scale
    weights = jnp.exp(scores) * keep_row[None, :]
    probs = (weights / jnp.sum(weights, axis=-1, keepdims=True)).astype(jnp.bfloat16)
    return jnp.dot(probs, valued, preferred_element_type=jnp.float32).astype(jnp.bfloat16)


def spatial_attention(stacked, keep_rows, attend):
    three, patches, columns = stacked.shape
    pairs = keep_rows.shape[0]
    split = stacked.reshape(3, patches, pairs, columns // pairs).transpose(2, 0, 1, 3)
    result = lax.map(attend, (split, keep_rows))
    return result.transpose(1, 0, 2).reshape(patches, columns)


def block_group(tokens, attended, w_so, w_gqkv, w_go):
    patches, groups, width = tokens.shape
    rows = patches * groups
    heads = H
    y_first = (
        tokens.reshape(rows, width).astype(jnp.float32)
        + jnp.dot(attended.reshape(rows, width), w_so, preferred_element_type=jnp.float32)
    ).astype(jnp.bfloat16)
    normed = rms_normalize(y_first)
    stacked = jnp.dot(normed, w_gqkv, preferred_element_type=jnp.float32).astype(jnp.bfloat16)
    stacked = stacked.reshape(patches, groups, 3, heads, width // heads)
    query = stacked[:, :, 0].astype(jnp.float32)
    keyed = stacked[:, :, 1].astype(jnp.float32)
    valued = stacked[:, :, 2].astype(jnp.float32)
    scale = (width // heads) ** (-0.5)
    scores = jnp.einsum("pgne,pkne->pngk", query, keyed) * scale
    weights = jnp.exp(scores)
    probs = (weights / jnp.sum(weights, axis=-1, keepdims=True)).astype(jnp.bfloat16)
    result = jnp.einsum("pngk,pkne->pgne", probs.astype(jnp.float32), valued).astype(jnp.bfloat16)
    result = result.reshape(rows, width)
    mixed = (
        y_first.astype(jnp.float32) + jnp.dot(result, w_go, preferred_element_type=jnp.float32)
    ).astype(jnp.bfloat16)
    return mixed.reshape(patches, groups, width)


def local_any(tokens, cotangent, w_sqkv, w_so, w_gqkv, w_go, keep):
    grid_size = lax.axis_size("grid")
    position = lax.axis_index("grid")
    full_sqkv, full_so, full_gqkv, full_go = (
        lax.all_gather(w_sqkv, "grid", axis=0, tiled=True),
        lax.all_gather(w_so, "grid", axis=0, tiled=True),
        lax.all_gather(w_gqkv, "grid", axis=0, tiled=True),
        lax.all_gather(w_go, "grid", axis=0, tiled=True),
    )
    stacked, pull_first = jax.vjp(partial(project_spatial, weight=full_sqkv), tokens)
    banded = lax.all_to_all(stacked, "grid", split_axis=2, concat_axis=1, tiled=True)
    pairs = G * H // grid_size
    pair_ids = position * pairs + jnp.arange(pairs, dtype=jnp.int32)
    select = (pair_ids[:, None] // H == jnp.arange(G, dtype=jnp.int32)[None, :]).astype(jnp.float32)
    keep_rows = jnp.dot(select, keep.astype(jnp.float32), precision=lax.Precision.HIGHEST)
    attend = jax.checkpoint(pair_attention)
    attended_bands, pull_spatial = jax.vjp(
        partial(spatial_attention, keep_rows=keep_rows, attend=attend), banded
    )
    attended = lax.all_to_all(attended_bands, "grid", split_axis=0, concat_axis=1, tiled=True)
    mixed, pull_group = jax.vjp(
        partial(block_group, w_so=full_so, w_gqkv=full_gqkv, w_go=full_go), tokens, attended
    )
    grad_direct, grad_attended = pull_group(cotangent)
    grad_bands = lax.all_to_all(grad_attended, "grid", split_axis=1, concat_axis=0, tiled=True)
    (grad_banded,) = pull_spatial(grad_bands)
    grad_stacked = lax.all_to_all(grad_banded, "grid", split_axis=1, concat_axis=2, tiled=True)
    (grad_first,) = pull_first(grad_stacked)
    return (mixed, grad_direct + grad_first)


F32 = jnp.float32
BF16 = jnp.bfloat16
LANES = 128
EPS = 1e-06


def nn(a, b):
    return lax.dot_general(a, b, (((1,), (0,)), ((), ())), preferred_element_type=F32)


def nt(a, b):
    return lax.dot_general(a, b, (((1,), (1,)), ((), ())), preferred_element_type=F32)


def tn(a, b):
    return lax.dot_general(a, b, (((0,), (0,)), ((), ())), preferred_element_type=F32)


def rms_parts(wide):
    inv = lax.rsqrt(jnp.mean(wide * wide, axis=-1, keepdims=True) + EPS)
    return inv, (wide * inv).astype(BF16)


def rms_pull(wide, inv, grad):
    inner = jnp.mean(grad * wide, axis=-1, keepdims=True)
    return grad * inv - wide * (inv * inv * inv * inner)


def halves(head):
    lane = lax.broadcasted_iota(jnp.int32, (1, LANES), 1)
    parts = []
    for index in range(LANES // head):
        parts.append((lane // head == index).astype(F32))
    return parts


def merge(selects, parts):
    total = parts[0] * selects[0]
    for select, part in zip(selects[1:], parts[1:]):
        total = total + part * select
    return total.astype(BF16)


def head_probs(query, keyed, select, mask, scale):
    scores = nt(query * select.astype(BF16), keyed) * scale
    weights = jnp.where(mask, jnp.exp(scores), 0.0)
    return weights * (1.0 / jnp.sum(weights, axis=-1, keepdims=True))


def head_pull(probs, query, keyed, valued, grad, select, scale):
    dprobs = nt(grad * select.astype(BF16), valued).astype(BF16).astype(F32)
    inner = jnp.sum(dprobs * probs, axis=-1, keepdims=True)
    dscores = (probs * (dprobs - inner) * scale).astype(BF16)
    return nn(dscores, keyed), tn(dscores, query), tn(probs.astype(BF16), grad)


def columns_of(qkv_ref, width, block):
    at = block * LANES
    return tuple(qkv_ref[:, part * width + at : part * width + at + LANES] for part in range(3))


def fetch(full_ref, held_ref, sems, order):
    width = held_ref.shape[2]
    copies = []
    for block in range(4):
        columns = full_ref.at[:, block * width : (block + 1) * width]
        copies.append(pltpu.make_async_copy(columns, held_ref.at[block], sems.at[block]))
    for block in order:
        copies[block].start()
    return copies


def project(normed, held_ref, copies, qkv_ref, tile):
    width = held_ref.shape[2]
    for part in range(3):
        copies[part].wait()
        for at in range(0, width, tile):
            columns = slice(part * width + at, part * width + at + tile)
            qkv_ref[:, columns] = nn(normed, held_ref[part, :, at : at + tile]).astype(BF16)


def project_pull(dqkv_ref, held_ref, out_ref, tile):
    width = held_ref.shape[2]
    for at in range(0, width, tile):
        total = nt(dqkv_ref[:, :width], held_ref[0, at : at + tile, :])
        for part in range(1, 3):
            columns = slice(part * width, (part + 1) * width)
            total = total + nt(dqkv_ref[:, columns], held_ref[part, at : at + tile, :])
        out_ref[:, at : at + tile] = total.astype(BF16)


def spatial_kernel(head, x_ref, full_ref, keep_ref, qkv_ref, y_ref, att_ref, held_ref, sems):
    copies = fetch(full_ref, held_ref, sems, (0, 1, 2, 3))
    width = x_ref.shape[1]
    _, normed = rms_parts(x_ref[...].astype(F32))
    tile = 512
    project(normed, held_ref, copies, qkv_ref, tile)
    rows = x_ref.shape[0]
    mask = jnp.broadcast_to(keep_ref[...], (rows, rows)) > 0.0
    selects = halves(head)
    scale = head ** (-0.5)
    for block in range(width // LANES):
        query, keyed, valued = columns_of(qkv_ref, width, block)
        parts = []
        for select in selects:
            probs = head_probs(query, keyed, select, mask, scale)
            parts.append(nn(probs.astype(BF16), valued))
        att_ref[:, block * LANES : (block + 1) * LANES] = merge(selects, parts)
    attended = att_ref[...]
    copies[3].wait()
    for at in range(0, width, tile):
        y_ref[:, at : at + tile] = (
            x_ref[:, at : at + tile].astype(F32) + nn(attended, held_ref[3, :, at : at + tile])
        ).astype(BF16)


def spatial_pull_kernel(
    head, dy_ref, x_ref, qkv_ref, keep_ref, full_ref, out_ref, datt_ref, dqkv_ref, held_ref, sems
):
    copies = fetch(full_ref, held_ref, sems, (3, 0, 1, 2))
    rows, width = x_ref.shape
    dy = dy_ref[...]
    tile = 512
    copies[3].wait()
    for at in range(0, width, tile):
        datt_ref[:, at : at + tile] = nt(dy, held_ref[3, at : at + tile, :]).astype(BF16)
    mask = jnp.broadcast_to(keep_ref[...], (rows, rows)) > 0.0
    selects = halves(head)
    scale = head ** (-0.5)
    for block in range(width // LANES):
        query, keyed, valued = columns_of(qkv_ref, width, block)
        at = block * LANES
        grad = datt_ref[:, at : at + LANES]
        pulled = []
        for select in selects:
            probs = head_probs(query, keyed, select, mask, scale)
            pulled.append(head_pull(probs, query, keyed, valued, grad, select, scale))
        for part in range(3):
            dqkv_ref[:, part * width + at : part * width + at + LANES] = merge(
                selects, [pull[part] for pull in pulled]
            )
    wide = x_ref[...].astype(F32)
    inv, _ = rms_parts(wide)
    for part in range(3):
        copies[part].wait()
    project_pull(dqkv_ref, held_ref, datt_ref, tile)
    first = rms_pull(wide, inv, datt_ref[...].astype(F32)).astype(BF16)
    out_ref[...] = dy + first


def group_kernel(
    head, patches, y_ref, c_ref, full_ref, mixed_ref, dy_ref, qkv_ref, att_ref, datt_ref, held_ref, sems
):
    copies = fetch(full_ref, held_ref, sems, (0, 1, 2, 3))
    rows, width = y_ref.shape
    groups = rows // patches
    row = lax.broadcasted_iota(jnp.int32, (rows, rows), 0)
    col = lax.broadcasted_iota(jnp.int32, (rows, rows), 1)
    turn = (col == (row % groups) * patches + row // groups).astype(F32).astype(BF16)
    mask = (row // groups) == (col // groups)
    y_first = nn(turn, y_ref[...])
    inv, normed = rms_parts(y_first)
    cot = c_ref[...]
    tile = 512
    project(normed, held_ref, copies, qkv_ref, tile)
    copies[3].wait()
    for at in range(0, width, tile):
        datt_ref[:, at : at + tile] = nt(cot, held_ref[3, at : at + tile, :]).astype(BF16)
    selects = halves(head)
    scale = head ** (-0.5)
    for block in range(width // LANES):
        query, keyed, valued = columns_of(qkv_ref, width, block)
        at = block * LANES
        grad = datt_ref[:, at : at + LANES]
        parts, pulled = [], []
        for select in selects:
            probs = head_probs(query, keyed, select, mask, scale)
            parts.append(nn(probs.astype(BF16), valued))
            pulled.append(head_pull(probs, query, keyed, valued, grad, select, scale))
        att_ref[:, at : at + LANES] = merge(selects, parts)
        for part in range(3):
            qkv_ref[:, part * width + at : part * width + at + LANES] = merge(
                selects, [pull[part] for pull in pulled]
            )
    attended = att_ref[...]
    for at in range(0, width, tile):
        mixed_ref[:, at : at + tile] = (
            y_first[:, at : at + tile] + nn(attended, held_ref[3, :, at : at + tile])
        ).astype(BF16)
    project_pull(qkv_ref, held_ref, datt_ref, tile)
    dy = cot + rms_pull(y_first, inv, datt_ref[...].astype(F32)).astype(BF16)
    dy_ref[...] = tn(turn, dy).astype(BF16)


def on_chip(kernel, weights, operands, outs, scratch, flops, moved):
    specs = [
        pl.BlockSpec(memory_space=pl.ANY)
        if operand is weights
        else pl.BlockSpec(operand.shape, lambda _: (0, 0), pipeline_mode=pl.Buffered(1))
        for operand in operands
    ]
    width = weights.shape[0]
    return pl.pallas_call(
        kernel,
        grid=(1,),
        in_specs=specs,
        out_specs=tuple(pl.BlockSpec(shape, lambda _: (0, 0)) for shape in outs),
        out_shape=tuple(jax.ShapeDtypeStruct(shape, BF16) for shape in outs),
        scratch_shapes=[pltpu.VMEM(shape, BF16) for shape in scratch]
        + [pltpu.VMEM((4, width, width), BF16), pltpu.SemaphoreType.DMA((4,))],
        cost_estimate=pl.CostEstimate(flops=flops, bytes_accessed=moved, transcendentals=0),
    )(*operands)


SPLIT = (2, 2, 2)


def gather_kernel(shard_ref, full_ref, send_sem, recv_sem, own_sem):
    count = lax.axis_size("grid")
    ny, nx, nc = SPLIT
    depth = count // (ny * nx * nc)
    part = lax.axis_index("parts")
    me = lax.axis_index("grid")
    core, x, y, z = me % 2, (me // 2) % 2, (me // 4) % 2, me // 8
    rows, columns = shard_ref.shape
    cuts = part_cuts(columns)

    def place(z, y, x, core):
        return ((z * ny + y) * nx + x) * nc + core

    def back(k):
        return (z + depth - k) % depth

    zs = [place((z + k) % depth, y, x, core) for k in range(depth)]
    xp, yp, cp = place(z, y, 1 - x, core), place(z, 1 - y, x, core), place(z, y, x, 1 - core)
    peers = zs[1:] + [xp, yp, cp]
    barrier = pltpu.get_barrier_semaphore()
    for peer in peers:
        pl.semaphore_signal(
            barrier, inc=1, device_id=(part, peer), device_id_type=pl.DeviceIdType.MESH
        )
    pl.semaphore_wait(barrier, len(peers))

    slots, sent = {}, []

    def slot(name):
        return slots.setdefault(name, len(slots))

    def region(half, owner):
        low, high = cuts[half]
        return full_ref.at[pl.ds(pl.multiple_of(owner * rows, rows), rows), low:high]

    def own(half):
        low, high = cuts[half]
        return shard_ref.at[:, low:high]

    def copy(name, half, owner, peer, source=None):
        at = slot(name)
        return pltpu.make_async_remote_copy(
            src_ref=region(half, owner) if source is None else source,
            dst_ref=region(half, owner),
            send_sem=send_sem.at[at],
            recv_sem=recv_sem.at[at],
            device_id=(part, peer),
            device_id_type=pl.DeviceIdType.MESH,
        )

    def send(name, half, owner, peer):
        source = own(half) if name[1] == "own" else None
        made = copy(name, half, owner, peer, source)
        made.start()
        sent.append(made)

    def arrive(name, half, owner):
        copy(name, half, owner, me).wait_recv()

    send(("cx", "own"), 2, me, xp)
    for k in range(1, depth):
        for half in range(2):
            send(("z", "own", half, k), half, me, zs[k])
    keep = pltpu.make_async_copy(shard_ref, full_ref.at[pl.ds(pl.multiple_of(me * rows, rows), rows), :], own_sem)
    keep.start()
    order = ((("y", yp), ("x", xp)), (("x", xp), ("y", yp)))

    def owner_of(half, k, first, second):
        cross_y, cross_x = (first, second) if half == 0 else (second, first)
        return place(back(k), 1 - y if cross_y else y, 1 - x if cross_x else x, core)

    def spread_line(k):
        tag = "own" if k == 0 else "line"
        for half in range(2):
            mine = owner_of(half, k, False, False)
            send(("first", tag, half, k), half, mine, order[half][0][1])
        for half in range(2):
            mine = owner_of(half, k, False, False)
            send(("second", tag, half, k, 0), half, mine, order[half][1][1])
            send(("core", tag, half, k, 0, 0), half, mine, cp)

    def spread_first(k):
        tag = "own" if k == 0 else "line"
        for half in range(2):
            got = owner_of(half, k, True, False)
            arrive(("first", tag, half, k), half, got)
            send(("second", "far", half, k, 1), half, got, order[half][1][1])
            send(("core", "far", half, k, 1, 0), half, got, cp)

    def spread_second(k, first):
        tag = "far" if first else ("own" if k == 0 else "line")
        for half in range(2):
            got = owner_of(half, k, bool(first), True)
            arrive(("second", tag, half, k, first), half, got)
            send(("core", "far", half, k, first, 1), half, got, cp)

    across = place(z, y, 1 - x, core)
    spread_line(0)
    send(("cy", "own", 0), 2, me, yp)
    send(("ccore", "own", 0, 0, 0), 2, me, cp)
    for k in range(1, depth):
        send(("cz", "own", k, 0, 0), 2, me, zs[k])
    arrive(("cx", "own"), 2, across)
    send(("cy", "far", 1), 2, across, yp)
    send(("ccore", "far", 0, 0, 1), 2, across, cp)
    for k in range(1, depth):
        send(("cz", "far", k, 0, 1), 2, across, zs[k])
    spread_first(0)
    for cross in range(2):
        got = place(z, 1 - y, 1 - x if cross else x, core)
        arrive(("cy", "far" if cross else "own", cross), 2, got)
        send(("ccore", "far", 0, 1, cross), 2, got, cp)
        for k in range(1, depth):
            send(("cz", "far", k, 1, cross), 2, got, zs[k])
    for k in range(1, depth):
        for half in range(2):
            arrive(("z", "own", half, k), half, place(back(k), y, x, core))
        spread_line(k)
        spread_second(k - 1, 0)
        if k > 1:
            spread_second(k - 2, 1)
        spread_first(k)
    spread_second(depth - 2, 1)
    spread_second(depth - 1, 0)
    for k in range(1, depth):
        for cross_y in range(2):
            for cross_x in range(2):
                tag = "far" if cross_y or cross_x else "own"
                got = place(back(k), 1 - y if cross_y else y, 1 - x if cross_x else x, core)
                arrive(("cz", tag, k, cross_y, cross_x), 2, got)
                send(("ccore", "far", k, cross_y, cross_x), 2, got, cp)
    spread_second(depth - 1, 1)
    for k in range(depth):
        for first in range(2):
            for second in range(2):
                tag = "far" if first or second else ("own" if k == 0 else "line")
                for half in range(2):
                    cross_y, cross_x = (first, second) if half == 0 else (second, first)
                    got = place(
                        back(k), 1 - y if cross_y else y, 1 - x if cross_x else x, 1 - core
                    )
                    arrive(("core", tag, half, k, first, second), half, got)
                got = place(back(k), 1 - y if first else y, 1 - x if second else x, 1 - core)
                tag = "far" if first or second or k else "own"
                arrive(("ccore", tag, k, first, second), 2, got)
    for made in sent:
        made.wait_send()
    keep.wait()


def part_cuts(columns):
    unit = columns // 32
    return ((0, 13 * unit), (13 * unit, 26 * unit), (26 * unit, columns))


def gather_weights(shard):
    rows, columns = shard.shape
    count = lax.axis_size("grid")
    depth = count // 8
    transfers = (2 * (depth - 1) + 14 * depth) + (3 + 4 * (depth - 1) + 4 * depth)
    return pl.pallas_call(
        gather_kernel,
        in_specs=[pl.BlockSpec(memory_space=pltpu.VMEM)],
        out_specs=pl.BlockSpec(memory_space=pl.ANY),
        out_shape=jax.ShapeDtypeStruct((rows * count, columns), BF16),
        scratch_shapes=[
            pltpu.SemaphoreType.DMA((transfers,)),
            pltpu.SemaphoreType.DMA((transfers,)),
            pltpu.SemaphoreType.DMA,
        ],
        compiler_params=pltpu.CompilerParams(collective_id=0, has_side_effects=True),
    )(shard)


def exchange(rows, grid_size):
    total, width = rows.shape
    split = rows.reshape(grid_size, total // grid_size, width)
    return lax.all_to_all(split, "grid", split_axis=0, concat_axis=0, tiled=True).reshape(
        total, width
    )


def local_bands(tokens, cotangent, w_sqkv, w_so, w_gqkv, w_go, keep):
    patches, groups, width = tokens.shape
    grid_size = lax.axis_size("grid")
    rows = patches * groups
    head = width // H
    position = lax.axis_index("grid")
    second = lax.all_gather(jnp.concatenate([w_gqkv, w_go], axis=1), "grid", axis=0, tiled=True)
    first = gather_weights(jnp.concatenate([w_sqkv, w_so], axis=1))
    keep_row = lax.dynamic_slice_in_dim(keep, position, 1, axis=0).astype(F32)
    weight = width * width
    product = 2 * rows * weight
    wide, flat = (rows, 3 * width), (rows, width)

    x = exchange(tokens.transpose(1, 0, 2).reshape(flat), grid_size)
    qkv, y_first = on_chip(
        partial(spatial_kernel, head),
        first,
        (x, first, keep_row),
        (wide, flat),
        (flat,),
        5 * product,
        8 * weight,
    )
    y_local = exchange(y_first, grid_size)
    mixed, dy_local = on_chip(
        partial(group_kernel, head, patches),
        second,
        (y_local, cotangent.reshape(flat), second),
        (flat, flat),
        (wide, flat, flat),
        10 * product,
        8 * weight,
    )
    dy = exchange(dy_local, grid_size)
    (grad,) = on_chip(
        partial(spatial_pull_kernel, head),
        first,
        (dy, x, qkv, keep_row, first),
        (flat,),
        (flat, wide),
        6 * product,
        8 * weight,
    )
    grad = exchange(grad, grid_size).reshape(groups, patches, width).transpose(1, 0, 2)
    return mixed.reshape(patches, groups, width), grad


def local(tokens, *rest):
    if lax.axis_size("grid") == tokens.shape[1]:
        return local_bands(tokens, *rest)
    return local_any(tokens, *rest)


def solution(mesh):
    placed = (
        P(("parts", "grid"), None, None),
        P(("parts", "grid"), None, None),
        P("grid", None),
        P("grid", None),
        P("grid", None),
        P("grid", None),
        P(None, "parts"),
    )
    return jax.shard_map(
        local,
        mesh=mesh,
        in_specs=placed,
        out_specs=(P(("parts", "grid"), None, None), P(("parts", "grid"), None, None)),
        check_vma=False,
    )
```
